32 devices in a mesh: rep: 4 (over z), dp: 8 (over y, x, core).
Axes of the slice: x: 2, y: 2, z: 4, core: 2. Of those that a mesh axis runs over, the one named last changes fastest.
Arguments:
- history: bfloat16 [8, 8192, 2048], P(None, ('rep', 'dp')), may hold values from -6 to 6
- stream_mix: float32 [8192, 32], P(('rep', 'dp')), may hold values from -3 to 3
- lengths: int32 [32], P(('rep', 'dp')), may hold values from 1 to 256, 5120 in all
- w_query: bfloat16 [2048, 2048], P('dp'), may hold values from -0.1875 to 0.1875
- w_key: bfloat16 [2048, 2048], P('dp'), may hold values from -0.1875 to 0.1875
- w_value: bfloat16 [2048, 2048], P('dp'), may hold values from -0.125 to 0.125
- w_output: bfloat16 [2048, 2048], P('dp'), may hold values from -0.5 to 0.5
- gain_query: bfloat16 [2048], P('dp'), may hold values from 0.25 to 1.75
- gain_key: bfloat16 [2048], P('dp'), may hold values from 0.25 to 1.75
- gain_value: bfloat16 [2048], P('dp'), may hold values from 0.25 to 1.75
- w_up: bfloat16 [2048, 8192], P('dp'), may hold values from -0.125 to 0.125
- w_down: bfloat16 [8192, 2048], P('dp'), may hold values from -0.0625 to 0.0625
- gain_mlp: bfloat16 [2048], P('dp'), may hold values from 0.25 to 1.75
- w_mix_in: bfloat16 [2048, 32], P('dp'), may hold values from -0.125 to 0.125
- w_mix_out: bfloat16 [32, 36], P('dp'), may hold values from -1 to 1
- gain_mix: bfloat16 [2048], P('dp'), may hold values from 0.25 to 1.75
- grad_block: bfloat16 [8192, 2048], P(('rep', 'dp')), may hold values from -6 to 6
- grad_next: float32 [8192, 36], P(('rep', 'dp')), may hold values from -6 to 6
Outputs:
- block_output: bfloat16 [8192, 2048], P(('rep', 'dp'))
- next_mix: float32 [8192, 36], P(('rep', 'dp'))
- grad_history: bfloat16 [8, 8192, 2048], P(None, ('rep', 'dp'))
- grad_stream_mix: float32 [8192, 32], P(('rep', 'dp'))
- grad_w_query: float32 [2048, 2048], P('dp')
- grad_w_key: float32 [2048, 2048], P('dp')
- grad_w_value: float32 [2048, 2048], P('dp')
- grad_w_output: float32 [2048, 2048], P('dp')
- grad_gain_query: float32 [2048], P('dp')
- grad_gain_key: float32 [2048], P('dp')
- grad_gain_value: float32 [2048], P('dp')
- grad_w_up: float32 [2048, 8192], P('dp')
- grad_w_down: float32 [8192, 2048], P('dp')
- grad_gain_mlp: float32 [2048], P('dp')
- grad_w_mix_in: float32 [2048, 32], P('dp')
- grad_w_mix_out: float32 [32, 36], P('dp')
- grad_gain_mix: float32 [2048], P('dp')
The draws below stay inside these ranges and needn't reach their ends.
Inputs may be any that keep to these rules, and one draw needn't show every extreme that they name: `lengths`: each slot's sequence fills it from its start; in every draw some slot holds exactly 256 valid tokens.
All inputs are finite; a program needn't handle non-finite values. No bound on the sum of `lengths` on one device may be relied on, other than what follows from the above.
Results may differ from the reference program's by a relative error of at most 0.02.
Values may be sent and summed in bfloat16 or wider, within the bound.
No kernel may reach another device: no remote copies, remote signals or barrier semaphores. Data moves between devices by JAX's collectives and lax.ppermute only.
A program may use at most 448 MiB of HBM per device.

```python
import math
import jax
import jax.numpy as jnp
import numpy as np
from jax import lax

D = 2048
HEADS = 16
HD = 128
FF = 8192
HIST = 8
STREAMS = 4
MIXH = 32
MIXOUT = 36
SLOT = 256
SLOTS = 32
TOKENS = 8192


def level_of(rng, dims, split, smallest, largest):
    loudness = 1.0
    for axis_at, blocks in split:
        heights = jax.random.uniform(jax.random.fold_in(jax.random.fold_in(rng, 6), axis_at), (blocks,), jnp.float32, smallest / len(split), largest / len(split))
        loudness = loudness * jnp.repeat(jnp.exp(heights), dims[axis_at] // blocks).reshape((-1,) + (1,) * (len(dims) - 1 - axis_at))
    return loudness


def split_up(amount, total, reach, skew):
    portions = [(1 << 20) // math.isqrt(rank ** skew) + 1 for rank in range(2, amount + 1)]
    spare, counts = total - reach - (amount - 1), [1] * (amount - 1)
    while spare > 0:
        free = [i for i in range(amount - 1) if counts[i] < reach]
        pool, remaining = sum([portions[i] for i in free]), spare
        for i in free:
            addition = min(reach - counts[i], max(1, remaining * portions[i] // pool), spare)
            counts[i] = counts[i] + addition
            spare = spare - addition
    return np.array([reach] + counts)


def ragged_sizes(own_key, count, total, limit, slope):
    if count == 2:
        one = jax.random.randint(own_key, (), max(1, total - limit), min(limit, total - 1) + 1)
        return jnp.stack([one, total - one])
    sizes = jnp.asarray(split_up(count, total, limit, slope), jnp.int32)
    couples = (count - 1) // 2
    source_of, taker = sizes[1:1 + 2 * couples:2], sizes[2:2 + 2 * couples:2]
    margin = jnp.minimum(source_of - 1, limit - taker)
    moved = jax.random.randint(jax.random.fold_in(own_key, 1), (couples,), 0, 1 << 20) % (margin + 1)
    sizes = sizes.at[1:1 + 2 * couples:2].set(source_of - moved).at[2:2 + 2 * couples:2].set(taker + moved)
    return sizes[jax.random.permutation(jax.random.fold_in(own_key, 2), count)]


def noise(key, dims, spread, most, shards=(), held_as=jnp.bfloat16):
    array = spread * jax.random.normal(key, dims, jnp.float32)
    if shards:
        array = array * level_of(key, dims, shards, -0.22, 0.18)
    return jnp.clip(array, -most, most).astype(held_as)


def setup_inputs(seed: int = 0) -> dict:
    streams_of = jax.random.split(jax.random.key(seed), 19)
    history = noise(streams_of[0], (HIST, TOKENS, D), 1.0, 6.0, ((1, 32),))
    stream_mix = noise(streams_of[1], (TOKENS, STREAMS * HIST), 0.5, 3.0, ((0, 32),), jnp.float32)
    lengths = ragged_sizes(streams_of[2], SLOTS, SLOTS * SLOT * 5 // 8, SLOT, 2).astype(jnp.int32)
    w_query = noise(streams_of[3], (D, D), (D // 2) ** -0.5, 0.1875, ((0, 8),))
    w_key = noise(streams_of[4], (D, D), (D // 2) ** -0.5, 0.1875, ((0, 8),))
    w_value = noise(streams_of[5], (D, D), D ** -0.5, 0.125, ((0, 8),))
    w_output = noise(streams_of[6], (D, D), (D // 16) ** -0.5, 0.5, ((0, 8),))
    gain_query = jnp.clip(1.0 + 0.15 * jax.random.normal(streams_of[7], (D,), jnp.float32), 0.25, 1.75).astype(jnp.bfloat16)
    gain_key = jnp.clip(1.0 + 0.15 * jax.random.normal(streams_of[8], (D,), jnp.float32), 0.25, 1.75).astype(jnp.bfloat16)
    gain_value = jnp.clip(1.0 + 0.15 * jax.random.normal(streams_of[9], (D,), jnp.float32), 0.25, 1.75).astype(jnp.bfloat16)
    w_up = noise(streams_of[10], (D, FF), D ** -0.5, 0.125, ((0, 8),))
    w_down = noise(streams_of[11], (FF, D), FF ** -0.5, 0.0625, ((0, 8),))
    gain_mlp = jnp.clip(1.0 + 0.15 * jax.random.normal(streams_of[12], (D,), jnp.float32), 0.25, 1.75).astype(jnp.bfloat16)
    w_mix_in = noise(streams_of[13], (D, MIXH), D ** -0.5, 0.125, ((0, 8),))
    w_mix_out = noise(streams_of[14], (MIXH, MIXOUT), MIXH ** -0.5, 1.0, ((0, 8),))
    gain_mix = jnp.clip(1.0 + 0.15 * jax.random.normal(streams_of[15], (D,), jnp.float32), 0.25, 1.75).astype(jnp.bfloat16)
    grad_block = noise(streams_of[16], (TOKENS, D), 1.0, 6.0, ((0, 32),))
    grad_next = noise(streams_of[17], (TOKENS, MIXOUT), 1.0, 6.0, ((0, 32),), jnp.float32)
    return dict(history=history, stream_mix=stream_mix, lengths=lengths, w_query=w_query, w_key=w_key, w_value=w_value, w_output=w_output, gain_query=gain_query, gain_key=gain_key, gain_value=gain_value, w_up=w_up, w_down=w_down, gain_mlp=gain_mlp, w_mix_in=w_mix_in, w_mix_out=w_mix_out, gain_mix=gain_mix, grad_block=grad_block, grad_next=grad_next)


@jax.custom_vjp
def low(v):
    return lax.optimization_barrier(v.astype(jnp.bfloat16)).astype(jnp.float32)

@jax.custom_vjp
def low_back(v):
    return v

def low_keep(v):
    return (low(v), None)

def low_pass(kept, grad):
    return (grad,)

def back_keep(v):
    return (v, None)

def back_low(kept, grad):
    return (low(grad),)
low.defvjp(low_keep, low_pass)
low_back.defvjp(back_keep, back_low)

def matmul(left, right):
    return jnp.dot(left, right, precision=lax.Precision.HIGHEST, preferred_element_type=jnp.float32)

def rms_scale(value, gain):
    return value * lax.rsqrt(lax.optimization_barrier(jnp.mean(value * value, axis=-1, keepdims=True)) + 1e-06) * gain

def rotary(heads_value):
    row_count = heads_value.shape[0]
    half_size = heads_value.shape[-1] // 2
    freqs = 10000.0 ** (-jnp.arange(half_size, dtype=jnp.float32) / half_size)
    angles = jnp.arange(row_count, dtype=jnp.float32)[:, None] * freqs[None, :]
    cos_part = jnp.cos(angles)[:, None, :]
    sin_part = jnp.sin(angles)[:, None, :]
    first_half = heads_value[..., :half_size]
    second_half = heads_value[..., half_size:]
    return jnp.concatenate([first_half * cos_part - second_half * sin_part, second_half * cos_part + first_half * sin_part], axis=-1)

def layer_forward(params, hist_seq, mix_seq, valid_count):
    w_query, w_key, w_value, w_output, gain_query, gain_key, gain_value, w_up, w_down, gain_mlp, w_mix_in, w_mix_out, gain_mix = params
    row_count = hist_seq.shape[1]
    weights_mix = mix_seq.reshape(row_count, STREAMS, HIST)
    streams = jnp.einsum('tsj,jtd->std', weights_mix, hist_seq, precision=lax.Precision.HIGHEST)
    normed_q = low(rms_scale(streams[0], gain_query))
    normed_k = low(rms_scale(streams[1], gain_key))
    normed_v = low(rms_scale(streams[2], gain_value))
    query = low_back(matmul(normed_q, w_query))
    keys = low_back(matmul(normed_k, w_key))
    values = low(low_back(matmul(normed_v, w_value)))
    query_rot = low(rotary(query.reshape(row_count, HEADS, HD)))
    keys_rot = low(rotary(keys.reshape(row_count, HEADS, HD)))
    value_heads = values.reshape(row_count, HEADS, HD)
    score_scale = HD ** (-0.5)
    scores = low_back(jnp.einsum('qhe,khe->hqk', query_rot, keys_rot, precision=lax.Precision.HIGHEST) * score_scale)
    position = jnp.arange(row_count, dtype=jnp.int32)
    allowed = (position[None, :] <= position[:, None]) & (position[None, :] < valid_count)
    scores = jnp.where(allowed[None], scores, -1e+30)
    probs = jax.nn.softmax(scores, axis=-1)
    mixed = low(low_back(jnp.einsum('hqk,khe->qhe', low(probs), value_heads, precision=lax.Precision.HIGHEST)))
    mixed = mixed.reshape(row_count, HEADS * HD)
    hidden = streams[3] + low_back(matmul(mixed, w_output))
    normed_m = low(rms_scale(hidden, gain_mlp))
    upper = low_back(matmul(normed_m, w_up))
    active = low(jax.nn.gelu(upper))
    block = hidden + low_back(matmul(active, w_down))
    normed_x = low(rms_scale(block, gain_mix))
    inner = low_back(matmul(normed_x, w_mix_in))
    logits = low_back(matmul(low(jax.nn.gelu(inner)), w_mix_out))
    row_keep = (position < valid_count).astype(jnp.float32)[:, None]
    return (block * row_keep, logits * row_keep)

def reference(history, stream_mix, lengths, w_query, w_key, w_value, w_output, gain_query, gain_key, gain_value, w_up, w_down, gain_mlp, w_mix_in, w_mix_out, gain_mix, grad_block, grad_next):
    params = tuple((item.astype(jnp.float32) for item in (w_query, w_key, w_value, w_output, gain_query, gain_key, gain_value, w_up, w_down, gain_mlp, w_mix_in, w_mix_out, gain_mix)))
    hist_all = jnp.moveaxis(history.reshape(HIST, SLOTS, SLOT, D), 1, 0)
    mix_all = stream_mix.reshape(SLOTS, SLOT, STREAMS * HIST)
    cot_block_all = grad_block.reshape(SLOTS, SLOT, D)
    cot_next_all = grad_next.reshape(SLOTS, SLOT, MIXOUT)

    def one_sequence(totals, inputs):
        hist_seq, mix_seq, valid_count, cot_block, cot_next = inputs
        hist_float = hist_seq.astype(jnp.float32)
        outputs, pullback = jax.vjp(lambda pars, hist_in, mix_in: layer_forward(pars, hist_in, mix_in, valid_count), params, hist_float, mix_seq)
        grads_params, grad_hist, grad_mix = pullback((cot_block.astype(jnp.float32), cot_next))
        totals = jax.tree.map(lambda first, second: first + second, totals, grads_params)
        return (totals, (outputs[0].astype(jnp.bfloat16), outputs[1], grad_hist.astype(jnp.bfloat16), grad_mix))
    zero_grads = tuple((jnp.zeros(item.shape, jnp.float32) for item in params))
    totals, stacked = lax.scan(one_sequence, zero_grads, (hist_all, mix_all, lengths.astype(jnp.int32), cot_block_all, cot_next_all))
    block_output = stacked[0].reshape(TOKENS, D)
    next_mix = stacked[1].reshape(TOKENS, MIXOUT)
    grad_history = jnp.moveaxis(stacked[2], 1, 0).reshape(HIST, TOKENS, D)
    grad_stream_mix = stacked[3].reshape(TOKENS, STREAMS * HIST)
    return (block_output, next_mix, grad_history, grad_stream_mix, totals[0], totals[1], totals[2], totals[3], totals[4], totals[5], totals[6], totals[7], totals[8], totals[9], totals[10], totals[11], totals[12])
```

```python
import functools

import jax
import jax.numpy as jnp
from jax import lax
from jax.experimental import pallas as pl
from jax.experimental.pallas import tpu as pltpu
from jax.sharding import PartitionSpec as P

HEADS = 16
HD = 128
HIST = 8
STREAMS = 4
MIXH = 32
MIXOUT = 36
F32 = jnp.float32
BF16 = jnp.bfloat16

ORDER = (0, 2, 4, 6, 1, 3, 5, 7)


def rms_scale(value, gain):
    return value * lax.rsqrt(jnp.mean(value * value, axis=-1, keepdims=True) + 1e-06) * gain


def rotary(heads_value):
    row_count = heads_value.shape[0]
    half_size = heads_value.shape[-1] // 2
    freqs = 10000.0 ** (-jnp.arange(half_size, dtype=jnp.float32) / half_size)
    angles = jnp.arange(row_count, dtype=jnp.float32)[:, None] * freqs[None, :]
    cos_part = jnp.cos(angles)[:, None, :]
    sin_part = jnp.sin(angles)[:, None, :]
    first_half = heads_value[..., :half_size]
    second_half = heads_value[..., half_size:]
    return jnp.concatenate(
        [
            first_half * cos_part - second_half * sin_part,
            second_half * cos_part + first_half * sin_part,
        ],
        axis=-1,
    )


def norm_back(value, gain, grad_normed):
    unused, pullback = jax.vjp(rms_scale, value, gain)
    return pullback(grad_normed)


def gelu_back(value, grad_value):
    unused, pullback = jax.vjp(jax.nn.gelu, value)
    return pullback(grad_value)[0]


def rotary_back(value, grad_value):
    unused, pullback = jax.vjp(rotary, value)
    return pullback(grad_value)[0]


def after(value, *earlier):
    return lax.optimization_barrier((value,) + earlier)[0]


class Group:
    def __init__(self, count, rep):
        self.count = count
        self.rep = rep
        self.fast = count == 8
        self.me = lax.axis_index("dp")
        self.chain = [None, None, None]

    def swap(self, value, k):
        return lax.ppermute(value, "dp", [(i, i ^ k) for i in range(self.count)])

    def blocks(self, value, axis):
        if not self.fast:
            return value
        size = value.shape[axis] // self.count
        return jnp.concatenate(
            [lax.dynamic_slice_in_dim(value, (self.me ^ k) * size, size, axis) for k in ORDER], axis
        )

    def natural(self, value, axis):
        if not self.fast:
            return value
        size = value.shape[axis] // self.count
        where = jnp.array([ORDER.index(k) for k in range(self.count)], jnp.int32)
        return jnp.concatenate(
            [
                lax.dynamic_slice_in_dim(value, where[self.me ^ j] * size, size, axis)
                for j in range(self.count)
            ],
            axis,
        )

    def gather_start(self, piece, between=()):
        axis = piece.ndim - 2
        half = piece.shape[axis] // 2
        from_x = self.swap(piece, 2)
        from_y = self.swap(piece, 4)
        if between:
            from_x, from_y = after(from_x, *between), after(from_y, *between)
        far_a = self.swap(from_y[..., :half, :], 2)
        far_b = self.swap(from_x[..., half:, :], 4)
        near = jnp.concatenate([piece, from_x, from_y], axis)
        return near, jnp.concatenate([far_a, far_b], axis), self.swap(near, 1)

    def gather(self, piece):
        if not self.fast:
            return lax.all_gather(piece, "dp", axis=0, tiled=True)
        near, far, other = self.gather_start(piece)
        return jnp.concatenate([near, far, other, self.swap(far, 1)], 0)

    def scatter_sum(self, same, other, earlier=()):
        if not self.fast:
            whole = jnp.concatenate([same, other], 0)
            return lax.psum_scatter(whole, "dp", scatter_dimension=0, tiled=True).astype(F32), ()
        rows = same.shape[0] // 4
        half = rows // 2
        chip = (same.astype(F32) + self.swap(other, 1).astype(F32)).astype(BF16)
        to_x = jnp.concatenate([chip[rows : rows + half], chip[3 * rows : 3 * rows + half]], 0)
        to_y = jnp.concatenate([chip[2 * rows + half : 3 * rows], chip[3 * rows + half :]], 0)
        if earlier:
            to_x, to_y = after(to_x, *earlier), after(to_y, *earlier)
        from_x = self.swap(to_x, 2)
        from_y = self.swap(to_y, 4)
        seen = (from_x, from_y)
        from_x, from_y = from_x.astype(F32), from_y.astype(F32)
        pass_y = (chip[2 * rows : 2 * rows + half].astype(F32) + from_x[half:]).astype(BF16)
        pass_x = (chip[rows + half : 2 * rows].astype(F32) + from_y[half:]).astype(BF16)
        own_a = chip[:half].astype(F32) + from_x[:half] + self.swap(pass_y, 4).astype(F32)
        own_b = chip[half:rows].astype(F32) + from_y[:half] + self.swap(pass_x, 2).astype(F32)
        return jnp.concatenate([own_a, own_b], 0), seen

    def gather_small(self, value):
        if not self.fast:
            return lax.all_gather(value, "dp", axis=0, tiled=False)
        value = value[None]
        for k in (1, 2, 4):
            value = jnp.concatenate([value, self.swap(value, k)], 0)
        return jnp.concatenate(
            [lax.dynamic_slice_in_dim(value, self.me ^ j, 1, 0) for j in range(self.count)], 0
        )

    def sum_all(self, value):
        if not self.fast or self.rep != 4:
            return lax.psum(value, ("rep", "dp"))
        for k in (1, 2, 4):
            value = value + self.swap(value, k)
        for k in (1, 2):
            value = value + lax.ppermute(value, "rep", [(i, i ^ k) for i in range(self.rep)])
        return value

    def exchange_columns(self, value):
        if not self.fast:
            return lax.all_to_all(value, "dp", split_axis=1, concat_axis=0, tiled=True)
        size = value.shape[1] // self.count
        pieces = []
        for k in ORDER:
            piece = lax.dynamic_slice_in_dim(value, (self.me ^ k) * size, size, 1)
            pieces.append(self.swap(piece, k) if k else piece)
        return self.natural(jnp.concatenate(pieces, 0), 0)

    def exchange_rows(self, value):
        size = value.shape[0] // self.count
        if not self.fast:
            whole = lax.all_to_all(value, "dp", split_axis=0, concat_axis=1, tiled=True)
            return jnp.split(whole, self.count, axis=1)
        pieces = []
        for k in ORDER:
            piece = lax.dynamic_slice_in_dim(value, (self.me ^ k) * size, size, 0)
            pieces.append(self.swap(piece, k) if k else piece)
        return pieces

    def link(self, value, stage, pairs):
        if self.chain[stage] is not None:
            value = after(value, self.chain[stage])
        moved = lax.ppermute(value, "rep", pairs)
        self.chain[stage] = moved
        return moved

    def rep_sum(self, value):
        if self.rep != 4:
            return lax.psum(value, "rep").astype(F32)
        place = lax.axis_index("rep")
        first = self.link(value, 0, [(0, 1), (3, 2)])
        half = lax.reduce_precision(value.astype(F32) + first.astype(F32), 8, 7)
        across = self.link(half.astype(BF16), 1, [(1, 2), (2, 1)])
        total = lax.reduce_precision(half + across.astype(F32), 8, 7)
        last = self.link(total.astype(BF16), 2, [(1, 0), (2, 3)])
        return jnp.where((place == 0) | (place == 3), last.astype(F32), total)


def forward_dot(value, pieces):
    block = value.shape[1] // 8
    starts, sizes = (0, 3, 4, 7), (3, 1, 3, 1)
    total = 0.0
    for piece, start, size in zip(pieces, starts, sizes):
        if piece is not None:
            part = value[:, start * block : (start + size) * block]
            total = total + jnp.dot(part, piece, preferred_element_type=F32)
    return total


def backward_dot(value, pieces):
    return jnp.concatenate(
        [jnp.einsum("te,de->td", value, piece, preferred_element_type=F32) for piece in pieces], 1
    )


def mix_block(mix, index):
    return mix[:, index : index + 1]


def streams_kernel(block, order, me_ref, history_ref, mix_ref, gain_ref, streams_ref, q_ref, k_ref, v_ref):
    mix = mix_ref[...]
    width = streams_ref.shape[2]
    squares = [0.0, 0.0, 0.0]
    for start in range(0, width, block):
        at = pl.ds(start, block)
        sums = [None] * STREAMS
        for j in range(HIST):
            past = history_ref[j, :, at].astype(F32)
            for s in range(STREAMS):
                term = mix_block(mix, s * HIST + j) * past
                sums[s] = term if sums[s] is None else sums[s] + term
        for s in range(STREAMS):
            streams_ref[s, :, at] = sums[s]
            if s < 3:
                squares[s] = squares[s] + jnp.sum(sums[s] * sums[s], axis=1, keepdims=True)
    scales = [lax.rsqrt(total / width + 1e-06) for total in squares]
    for s, out_ref in enumerate((q_ref, k_ref, v_ref)):
        for place, k in enumerate(order):
            at = pl.ds(pl.multiple_of((me_ref[0] ^ k) * block, block), block)
            normed = streams_ref[s, :, at] * scales[s] * gain_ref[s : s + 1, at]
            out_ref[:, place * block : (place + 1) * block] = normed.astype(BF16)


def mixed_streams(me, order, history, stream_mix, gains):
    hist, rows, width = history.shape
    tile = 32
    token = pl.BlockSpec((tile, width), lambda i, me: (i, 0))
    out = jax.ShapeDtypeStruct((rows, width), BF16)
    return pl.pallas_call(
        functools.partial(streams_kernel, width // len(order), order),
        grid_spec=pltpu.PrefetchScalarGridSpec(
            num_scalar_prefetch=1,
            grid=(rows // tile,),
            in_specs=[
                pl.BlockSpec((hist, tile, width), lambda i, me: (0, i, 0)),
                pl.BlockSpec((tile, STREAMS * HIST), lambda i, me: (i, 0)),
                pl.BlockSpec((3, width), lambda i, me: (0, 0)),
            ],
            out_specs=[
                pl.BlockSpec((STREAMS, tile, width), lambda i, me: (0, i, 0)),
                token,
                token,
                token,
            ],
        ),
        out_shape=[jax.ShapeDtypeStruct((STREAMS, rows, width), F32), out, out, out],
        cost_estimate=pl.CostEstimate(
            flops=2 * STREAMS * HIST * rows * width,
            bytes_accessed=rows * width * (2 * hist + 4 * STREAMS + 6),
            transcendentals=0,
        ),
        compiler_params=pltpu.CompilerParams(vmem_limit_bytes=32 * 1024 * 1024),
        name="streams",
    )(me, history, stream_mix, gains)


def streams_back_kernel(
    block, order, me_ref, history_ref, mix_ref, gain_ref, streams_ref, q_ref, k_ref, v_ref, rest_ref,
    history_out, mix_out, gain_out, sums_ref, gain_sums,
):
    mix = mix_ref[...]
    rows, width = rest_ref.shape
    grads = (q_ref, k_ref, v_ref)
    scales, shifts = [], []
    for s in range(3):
        squares, cross = 0.0, 0.0
        for place, k in enumerate(order):
            at = pl.ds(pl.multiple_of((me_ref[0] ^ k) * block, block), block)
            value = streams_ref[s, :, at]
            grad = grads[s][:, place * block : (place + 1) * block] * gain_ref[s : s + 1, at]
            squares = squares + jnp.sum(value * value, axis=1, keepdims=True)
            cross = cross + jnp.sum(value * grad, axis=1, keepdims=True)
        scale = lax.rsqrt(squares / width + 1e-06)
        scales.append(scale)
        shifts.append(scale * scale * scale * (cross / width))
    sums_ref[...] = jnp.zeros_like(sums_ref)

    @pl.when(pl.program_id(0) == 0)
    def _():
        gain_sums[...] = jnp.zeros_like(gain_sums)

    for place, k in enumerate(order):
        for part in range(0, block, 128):
            lane = place * block + part
            at = pl.ds(pl.multiple_of((me_ref[0] ^ k) * block + part, 128), 128)
            backs = []
            for s in range(3):
                value = streams_ref[s, :, at]
                raw = grads[s][:, lane : lane + 128]
                grad = raw * gain_ref[s : s + 1, at]
                over = (raw * value * scales[s]).reshape(rows // 8, 8, 128)
                gain_sums[s, :, at] += jnp.sum(over, axis=0)
                backs.append(grad * scales[s] - value * shifts[s])
            backs.append(rest_ref[:, at])
            for j in range(HIST):
                past = history_ref[j, :, at].astype(F32)
                total = None
                for s in range(STREAMS):
                    term = mix_block(mix, s * HIST + j) * backs[s]
                    total = term if total is None else total + term
                    sums_ref[s * HIST + j] += backs[s] * past
                history_out[j, :, at] = total.astype(BF16)
    for index in range(STREAMS * HIST):
        mix_out[:, index : index + 1] = jnp.sum(sums_ref[index], axis=1, keepdims=True)

    @pl.when(pl.program_id(0) == pl.num_programs(0) - 1)
    def _():
        gain_out[...] = jnp.sum(gain_sums[...], axis=1)


def streams_back(me, order, history, stream_mix, gains, streams, d_q, d_k, d_v, d_rest):
    hist, rows, width = history.shape
    tile = 32
    token = pl.BlockSpec((tile, width), lambda i, me: (i, 0))
    stored = pl.BlockSpec((hist, tile, width), lambda i, me: (0, i, 0))
    weight = pl.BlockSpec((tile, STREAMS * HIST), lambda i, me: (i, 0))
    return pl.pallas_call(
        functools.partial(streams_back_kernel, width // len(order), order),
        grid_spec=pltpu.PrefetchScalarGridSpec(
            num_scalar_prefetch=1,
            grid=(rows // tile,),
            in_specs=[
                stored,
                weight,
                pl.BlockSpec((3, width), lambda i, me: (0, 0)),
                pl.BlockSpec((3, tile, width), lambda i, me: (0, i, 0)),
                token,
                token,
                token,
                token,
            ],
            out_specs=[stored, weight, pl.BlockSpec((3, width), lambda i, me: (0, 0))],
            scratch_shapes=[
                pltpu.VMEM((STREAMS * HIST, tile, 128), F32),
                pltpu.VMEM((3, 8, width), F32),
            ],
        ),
        out_shape=[
            jax.ShapeDtypeStruct(history.shape, BF16),
            jax.ShapeDtypeStruct((rows, STREAMS * HIST), F32),
            jax.ShapeDtypeStruct((3, width), F32),
        ],
        cost_estimate=pl.CostEstimate(
            flops=4 * STREAMS * HIST * rows * width,
            bytes_accessed=rows * width * (4 * hist + 28),
            transcendentals=0,
        ),
        compiler_params=pltpu.CompilerParams(vmem_limit_bytes=32 * 1024 * 1024),
        name="streams_back",
    )(me, history, stream_mix, gains, streams, d_q, d_k, d_v, d_rest)


def body(
    rep,
    count,
    history,
    stream_mix,
    lengths,
    w_query,
    w_key,
    w_value,
    w_output,
    gain_query,
    gain_key,
    gain_value,
    w_up,
    w_down,
    gain_mlp,
    w_mix_in,
    w_mix_out,
    gain_mix,
    grad_block,
    grad_next,
):
    group = Group(count, rep)
    me = group.me
    row_count = history.shape[1]
    width = history.shape[2]
    shard = width // count
    valid_count = lengths[0]
    position = jnp.arange(row_count, dtype=jnp.int32)
    row_keep = (position < valid_count).astype(F32)[:, None]
    score_scale = HD ** (-0.5)

    out_shard = w_mix_out.reshape(-1)
    out_row = jnp.zeros((shard,), BF16).at[: out_shard.shape[0]].set(out_shard)
    small = jnp.concatenate(
        [
            jnp.stack([gain_query, gain_key, gain_value, gain_mlp, gain_mix, out_row]),
            w_mix_in.T,
        ],
        0,
    )
    small = group.gather_small(small)
    gains = small[:, :5].transpose(1, 0, 2).reshape(5, width).astype(F32)
    full_gain_q, full_gain_k, full_gain_v, full_gain_m, full_gain_x = (gains[i] for i in range(5))
    full_mix_out = small[:, 5, : out_shard.shape[0]].reshape(MIXH, MIXOUT)
    full_mix_in = small[:, 6:].transpose(1, 0, 2).reshape(MIXH, width)

    order = ORDER if group.fast else tuple(range(8))
    place = (me if group.fast else jnp.zeros_like(me)).astype(jnp.int32)[None]
    streams, normed_q, normed_k, normed_v = mixed_streams(
        place, order, history, stream_mix, gains[:3]
    )
    three = jnp.stack([w_query, w_key, w_value])
    normed = (normed_q, normed_k, normed_v)
    if group.fast:
        near, far, near_other = group.gather_start(three, (normed_q,))
        early = [
            forward_dot(normed[i], (near[i], None, near_other[i], None)) for i in range(3)
        ]
        far_other = group.swap(after(far, *early), 1)
        query, keys, values = (
            early[i] + forward_dot(normed[i], (None, far[i], None, far_other[i])) for i in range(3)
        )
        full_query, full_key, full_value = (
            (near[i], far[i], near_other[i], far_other[i]) for i in range(3)
        )
        w_output, w_up = after(w_output, far), after(w_up, far)
    else:
        three = lax.all_gather(three, "dp", axis=1, tiled=True)
        query, keys, values = (
            jnp.dot(normed[i], three[i], preferred_element_type=F32) for i in range(3)
        )
        full_query, full_key, full_value = ((three[i],) for i in range(3))
    full_output = lax.all_gather(w_output, "dp", axis=0, tiled=True)
    up_cols = group.exchange_columns(w_up)
    query = query.reshape(row_count, HEADS, HD)
    keys = keys.reshape(row_count, HEADS, HD)
    value_heads = values.astype(BF16).reshape(row_count, HEADS, HD)
    query_rot = rotary(query).astype(BF16)
    keys_rot = rotary(keys).astype(BF16)
    raw_scores = (
        jnp.einsum("qhe,khe->hqk", query_rot, keys_rot, preferred_element_type=F32) * score_scale
    )
    allowed = (position[None, :] <= position[:, None]) & (position[None, :] < valid_count)
    scores = jnp.where(allowed[None], raw_scores, -1e30)
    row_max = jnp.max(scores, axis=-1, keepdims=True)
    weights = jnp.exp(scores - row_max)
    probs = weights / jnp.sum(weights, axis=-1, keepdims=True)
    probs_low = probs.astype(BF16)
    mixed = (
        jnp.einsum("hqk,khe->qhe", probs_low, value_heads, preferred_element_type=F32)
        .astype(BF16)
        .reshape(row_count, HEADS * HD)
    )
    hidden = streams[3] + jnp.dot(mixed, full_output, preferred_element_type=F32)

    normed_m = rms_scale(hidden, full_gain_m).astype(BF16)
    normed_all = group.gather(normed_m)
    middle = normed_all.shape[0] // 2
    upper = jnp.dot(normed_all, up_cols, preferred_element_type=F32)
    active, slope = jax.vjp(jax.nn.gelu, upper)
    slope = slope(jnp.ones_like(upper))[0]
    active, slope = lax.optimization_barrier((active.astype(BF16), slope))
    part_other = jnp.dot(active[middle:], w_down, preferred_element_type=F32).astype(BF16)
    part_same = jnp.dot(active[:middle], w_down, preferred_element_type=F32).astype(BF16)
    block = hidden + group.scatter_sum(part_same, part_other)[0]

    normed_x = rms_scale(block, full_gain_x).astype(BF16)
    inner = jnp.einsum("td,kd->tk", normed_x, full_mix_in, preferred_element_type=F32)
    inner_act = jax.nn.gelu(inner).astype(BF16)
    logits = jnp.dot(inner_act, full_mix_out, preferred_element_type=F32)
    block_output = (block * row_keep).astype(BF16)
    next_mix = logits * row_keep
    d_logits = (grad_next * row_keep).astype(BF16)
    grad_mix_out = jnp.einsum("tk,to->ko", inner_act, d_logits, preferred_element_type=F32)
    d_inner_act = jnp.einsum("to,ko->tk", d_logits, full_mix_out, preferred_element_type=F32)
    d_inner = gelu_back(inner, d_inner_act).astype(BF16)
    grad_mix_in = jnp.einsum("tk,td->kd", d_inner, normed_x, preferred_element_type=F32)
    d_normed_x = jnp.dot(d_inner, full_mix_in, preferred_element_type=F32)
    d_block_norm, grad_gain_x = norm_back(block, full_gain_x, d_normed_x)
    d_block = grad_block.astype(F32) * row_keep + d_block_norm

    d_block_low = d_block.astype(BF16)
    d_block_all = group.gather(d_block_low)
    grad_down = jnp.einsum("tf,td->fd", active, d_block_all, preferred_element_type=F32)
    grad_down = grad_down.astype(BF16)
    d_active = jnp.einsum(
        "td,fd->tf", after(d_block_all, grad_down), w_down, preferred_element_type=F32
    )
    d_upper = (slope * d_active).astype(BF16)
    back_other = jnp.einsum("tf,df->td", d_upper[middle:], up_cols, preferred_element_type=F32)
    back_same = jnp.einsum("tf,df->td", d_upper[:middle], up_cols, preferred_element_type=F32)
    back_same, back_other = back_same.astype(BF16), back_other.astype(BF16)
    d_normed_m, seen = group.scatter_sum(back_same, back_other)
    grad_up = jnp.einsum(
        "td,tf->df", after(normed_all, back_same), d_upper, preferred_element_type=F32
    ).astype(BF16)
    up_pieces = group.exchange_rows(after(grad_up, *seen) if seen else grad_up)
    d_hidden_norm, grad_gain_m = norm_back(hidden, full_gain_m, d_normed_m)
    d_hidden = d_block + d_hidden_norm

    d_hidden_low = d_hidden.astype(BF16)

    half_width = width // 2

    def weight_grad(inputs, outputs, earlier):
        def rows(columns):
            return jnp.einsum("td,te->de", columns, outputs, preferred_element_type=F32).astype(BF16)

        other = rows(inputs[:, half_width:])
        same = rows(inputs[:, :half_width])
        own, seen = group.scatter_sum(same, other, earlier)
        return own.astype(BF16), seen

    part_output, seen = weight_grad(group.blocks(mixed, 1), d_hidden_low, ())
    d_mixed = jnp.einsum("te,de->td", d_hidden_low, full_output, preferred_element_type=F32)
    d_mixed = d_mixed.astype(BF16).reshape(row_count, HEADS, HD)
    d_probs = jnp.einsum("qhe,khe->hqk", d_mixed, value_heads, preferred_element_type=F32)
    d_values = jnp.einsum("hqk,qhe->khe", probs_low, d_mixed, preferred_element_type=F32)
    row_delta = jnp.sum(probs * d_probs, axis=-1, keepdims=True)
    d_scores = (probs * (d_probs - row_delta)).astype(BF16)
    d_query_rot = (
        jnp.einsum("hqk,khe->qhe", d_scores, keys_rot, preferred_element_type=F32) * score_scale
    )
    d_keys_rot = (
        jnp.einsum("hqk,qhe->khe", d_scores, query_rot, preferred_element_type=F32) * score_scale
    )
    d_query = rotary_back(query, d_query_rot).astype(BF16).reshape(row_count, HEADS * HD)
    d_keys = rotary_back(keys, d_keys_rot).astype(BF16).reshape(row_count, HEADS * HD)
    d_values = d_values.astype(BF16).reshape(row_count, HEADS * HD)
    part_value, seen = weight_grad(normed_v, d_values, seen)
    part_query, seen = weight_grad(normed_q, d_query, seen)
    part_key, seen = weight_grad(normed_k, d_keys, seen)
    out_down = lax.psum(grad_down, "rep")
    per = count // 2
    up_sums = [group.rep_sum(jnp.concatenate(up_pieces[i : i + per], 1)) for i in (0, per)]
    out_up = group.natural(jnp.concatenate(up_sums, 1), 1)
    grad_output, grad_value = jnp.split(
        lax.psum(after(jnp.concatenate([part_output, part_value], 0), out_down), "rep"), 2
    )
    grad_query = group.rep_sum(part_query)
    grad_key = group.rep_sum(part_key)
    out_down = after(out_down, part_key)

    grad_history, grad_stream_mix, grad_gains = streams_back(
        place,
        order,
        history,
        stream_mix,
        gains[:3],
        streams,
        backward_dot(d_query, full_query),
        backward_dot(d_keys, full_key),
        backward_dot(d_values, full_value),
        d_hidden,
    )

    flat_out = grad_mix_out.reshape(-1)
    out_grad_row = jnp.zeros((width,), F32).at[: flat_out.shape[0]].set(flat_out)
    early = jnp.concatenate(
        [jnp.stack([grad_gain_x, grad_gain_m, out_grad_row]), grad_mix_in], 0
    )
    early = group.sum_all(early)
    late = group.sum_all(grad_gains)
    own_early = lax.dynamic_slice_in_dim(early, me * shard, shard, 1)
    own_late = lax.dynamic_slice_in_dim(late, me * shard, shard, 1)
    rows_out = MIXH // count
    own_mix_out = lax.dynamic_slice_in_dim(early[2], me * rows_out * MIXOUT, rows_out * MIXOUT, 0)

    return (
        block_output,
        next_mix,
        grad_history,
        grad_stream_mix,
        grad_query,
        grad_key,
        grad_value.astype(F32),
        grad_output.astype(F32),
        own_late[0],
        own_late[1],
        own_late[2],
        out_up,
        out_down.astype(F32),
        own_early[1],
        own_early[3:].T,
        own_mix_out.reshape(rows_out, MIXOUT),
        own_early[0],
    )


def solution(mesh):
    rep, count = mesh.shape["rep"], mesh.shape["dp"]

    def step(*args):
        return body(rep, count, *args)

    return jax.shard_map(
        step,
        mesh=mesh,
        in_specs=(
            P(None, ("rep", "dp"), None),
            P(("rep", "dp"), None),
            P(("rep", "dp")),
            P("dp", None),
            P("dp", None),
            P("dp", None),
            P("dp", None),
            P("dp"),
            P("dp"),
            P("dp"),
            P("dp", None),
            P("dp", None),
            P("dp"),
            P("dp", None),
            P("dp", None),
            P("dp"),
            P(("rep", "dp"), None),
            P(("rep", "dp"), None),
        ),
        out_specs=(
            P(("rep", "dp"), None),
            P(("rep", "dp"), None),
            P(None, ("rep", "dp"), None),
            P(("rep", "dp"), None),
            P("dp", None),
            P("dp", None),
            P("dp", None),
            P("dp", None),
            P("dp"),
            P("dp"),
            P("dp"),
            P("dp", None),
            P("dp", None),
            P("dp"),
            P("dp", None),
            P("dp", None),
            P("dp"),
        ),
        check_vma=False,
    )
```
